32 devices in a mesh: rep: 2 (over x), exp: 16 (over z, y, core).
Axes of the slice: x: 2, y: 2, z: 4, core: 2. Of those that a mesh axis runs over, the one named last changes fastest.
Arguments:
- tokens: bfloat16 [1, 128, 7168], P(None, 'exp', 'rep'), may hold values from -6 to 6
- gate_up: bfloat16 [16, 7168, 2, 2048], P('exp', 'rep'), may hold values from -0.09375 to 0.09375
- w_down: bfloat16 [16, 2048, 7168], P('exp', None, 'rep'), may hold values from -0.125 to 0.125
- routes: int32 [1, 128, 8], P(None, 'exp'), may hold values from 0 to 15, all different within a row; in each aligned block of 8 rows (0 to 7, 8 to 15, ..., all dimensions but the last counted through in order) at most 8 rows name the same one
- gates: float32 [1, 128, 8], P(None, 'exp'), may hold values from 0.05 to 1
Outputs:
- mixed_out: bfloat16 [1, 128, 7168], P(None, 'exp', 'rep')
The draws below stay inside these ranges and needn't reach their ends.
Inputs may be any that keep to these rules, and one draw needn't show every extreme that they name: `routes`: within one step, the 8 tokens of one index of exp name any expert at most 8 times, a bound that some block reaches.
All inputs are finite; a program needn't handle non-finite values.
Results may differ from the reference program's by a relative error of at most 0.024.
Values may be sent and summed in bfloat16 or wider, within the bound.
A program may use at most 192 MiB of HBM per device.

```python
import math
import jax
import jax.numpy as jnp
import numpy as np
from jax import lax

D = 7168
FF = 2048
TOP = 8
TOK_DEV = 8
STEPS = 1
EXPERTS = 16
TOKENS = 128
CAP = 8
N_REP = 2
N_EXP = 16


def raised(array, own_key, source, target, parts, factor):
    owner, partner = [(jnp.arange(array.shape[dim]) // (array.shape[dim] // parts)).reshape([-1 if axis == dim else 1 for axis in range(array.ndim)]) for dim in (source, target)]
    chosen = jax.random.permutation(own_key, parts)[partner]
    strong = (owner == chosen) | (owner == (partner + parts // 2) % parts)
    return jnp.where(strong, factor * array, array)


def levels(key, shape, pieces, low, high):
    gain, own = 1.0, jax.random.fold_in(key, 6)
    for axis_at, shards_of in pieces:
        draws = jnp.exp(jax.random.uniform(jax.random.fold_in(own, axis_at), (shards_of,), jnp.float32, low / len(pieces), high / len(pieces)))
        gain = gain * jnp.repeat(draws, shape[axis_at] // shards_of).reshape([-1 if axis == axis_at else 1 for axis in range(len(shape))])
    return gain


def shared_out(key, own, number, rows, amount, top, limit, lean):
    order = jax.random.permutation(key, amount)
    heavy_load, common = portions_of(amount, rows * top, limit, lean, True), portions_of(amount, rows * top, limit, lean, False)
    places = jnp.arange(amount)

    def named(lengths, rotation):
        used = int((lengths > 0).sum())
        fixed = max(1, used // 4)
        shifted = fixed + (places - fixed + rotation * (used - fixed)) % max(1, amount - fixed)
        return jnp.zeros((amount,), jnp.int32).at[order[jnp.where(places < fixed, places, shifted)]].set(jnp.asarray(lengths, jnp.int32))

    lengths = jnp.where(number % 4 == 0, named(heavy_load, number // 4), named(common, number - number // 4 - 1))
    mixed = jax.random.permutation(jax.random.fold_in(own, 3), amount)
    source_of, taker = mixed[0:amount // 2 * 2:2], mixed[1:amount // 2 * 2:2]
    slack = jnp.minimum(lengths[source_of] - 1, limit - lengths[taker]) // 2
    slack = jnp.where((source_of == order[0]) | (taker == order[0]) | (lengths[taker] == 0), 0, jnp.maximum(slack, 0))
    shifted = jax.random.randint(jax.random.fold_in(own, 4), (amount // 2,), 0, 1 << 20) % (slack + 1)
    lengths = lengths.at[source_of].add(-shifted).at[taker].add(shifted)
    items = jnp.searchsorted(jnp.cumsum(lengths), jnp.arange(rows * top), side="right").astype(jnp.int32)
    table = items.reshape(top, rows).T
    table = table[jax.random.permutation(jax.random.fold_in(own, 1), rows)]
    rotation = jax.random.randint(jax.random.fold_in(own, 2), (rows, 1), 0, top)
    return jnp.take_along_axis(table, (jnp.arange(top)[None, :] + rotation) % top, axis=1)


def portions_of(amount, total, limit, slope, full):
    loads = [(1 << 20) // math.isqrt(rank ** slope) + 1 for rank in range(1, amount + 1)]
    largest = limit if full else min(limit, max(-(-total // amount), total * loads[0] // sum(loads)))
    least = 1 if total - largest >= amount - 1 else 0
    counts, surplus = [largest] + [least] * (amount - 1), total - largest - least * (amount - 1)
    while surplus > 0:
        movable = [i for i in range(1, amount) if counts[i] < largest] or [i for i in range(1, amount) if counts[i] < limit]
        mass, remaining = sum([loads[i] for i in movable]), surplus
        for i in movable:
            addition = min(limit - counts[i], max(1, remaining * loads[i] // mass), surplus)
            counts[i] = counts[i] + addition
            surplus = surplus - addition
    return np.array(counts)


def normal_values(rng, dims, spread, limit, split=(), kind=jnp.bfloat16):
    drawn = jax.random.normal(rng, dims, jnp.float32) * spread
    if len(split) > 0:
        drawn = levels(rng, dims, split, -0.22, 0.18) * drawn
    return jnp.clip(drawn, min=-limit, max=limit).astype(kind)


def heavy_noise(own_key, dims, width, bound, cuts, heavy, kind=jnp.bfloat16):
    result = width * jax.random.normal(own_key, dims, jnp.float32)
    if cuts:
        result = result * levels(own_key, dims, cuts, -0.22, 0.18)
    return jnp.clip(raised(result, jax.random.fold_in(own_key, 3), *heavy), -bound, bound).astype(kind)


def setup_inputs(seed: int = 0) -> dict:
    key_list = jax.random.split(jax.random.key(seed), 6)
    tokens = normal_values(key_list[0], (STEPS, TOKENS, D), 1.0, 6.0, ((1, 16), (2, 2)))
    gate_up = heavy_noise(key_list[1], (EXPERTS, D, 2, FF), D ** -0.5, 0.09375, ((0, 16), (1, 2)), (1, 3, 2, 2.0))
    w_down = normal_values(key_list[2], (EXPERTS, FF, D), FF ** -0.5, 0.125, ((0, 16), (2, 2)))
    routes_keys = jax.random.split(jax.random.fold_in(key_list[3], 1), STEPS * TOKENS // TOK_DEV)
    routes_turns = jax.random.permutation(jax.random.fold_in(key_list[3], 3), STEPS * TOKENS // TOK_DEV)
    routes = jax.vmap(lambda own, number: shared_out(jax.random.fold_in(key_list[3], 2), own, number, TOK_DEV, EXPERTS, TOP, CAP, 2))(routes_keys, routes_turns).reshape((STEPS, TOKENS, TOP))
    gates = jnp.clip(jnp.exp(math.log(1.0) - 2.9957323 * jax.random.uniform(key_list[4], (STEPS, TOKENS, TOP), jnp.float32) ** levels(key_list[4], (STEPS, TOKENS, TOP), ((1, 16),), -0.2, 0.2)), 0.05, 1.0)
    return dict(tokens=tokens, gate_up=gate_up, w_down=w_down, routes=routes, gates=gates)


def reference(tokens, gate_up, w_down, routes, gates):
    steps_all, tokens_all, model_width = tokens.shape
    top_count = routes.shape[2]
    experts = gate_up.shape[0]
    hidden_units = w_down.shape[1]
    slab_width = model_width // N_REP
    row_count = N_EXP * CAP
    weights_in = gate_up.reshape(experts, N_REP, slab_width, 2 * hidden_units)

    def one_step(step_index):
        expert_ids = routes[step_index]
        features = tokens[step_index]
        onehot = (expert_ids[:, :, None] == jnp.arange(experts, dtype=jnp.int32)).astype(jnp.int32)
        flat_hot = onehot.reshape(N_EXP, TOK_DEV * top_count, experts)
        before = (jnp.cumsum(flat_hot, axis=1) - flat_hot).astype(jnp.int32)
        slot_rank = jnp.sum(before * flat_hot, axis=2).astype(jnp.int32).reshape(tokens_all, top_count)
        block_index = (jnp.arange(tokens_all, dtype=jnp.int32) // TOK_DEV)[:, None]
        slot_row = (block_index * CAP + slot_rank).astype(jnp.int32)
        token_index = jnp.broadcast_to(jnp.arange(tokens_all, dtype=jnp.int32)[:, None], expert_ids.shape)
        owner_table = jnp.full((experts, row_count), tokens_all, jnp.int32)
        owner_table = owner_table.at[expert_ids.reshape(-1), slot_row.reshape(-1)].set(token_index.reshape(-1))
        padded = jnp.concatenate([features, jnp.zeros((1, model_width), features.dtype)], axis=0)

        def expert_fn(expert_index):
            chosen = padded[owner_table[expert_index]].reshape(row_count, N_REP, slab_width).astype(jnp.float32)
            partials = jnp.einsum("rnf,nfh->nrh", chosen, weights_in[expert_index].astype(jnp.float32))
            partials = lax.optimization_barrier(partials.astype(jnp.bfloat16)).astype(jnp.float32)
            summed = jnp.sum(partials, axis=0)
            gate_part = summed[:, :hidden_units]
            up_part = summed[:, hidden_units:]
            hidden = (jax.nn.silu(gate_part) * up_part).astype(jnp.bfloat16)
            return jnp.dot(hidden, w_down[expert_index], preferred_element_type=jnp.float32).astype(jnp.bfloat16)

        results = lax.map(expert_fn, jnp.arange(experts, dtype=jnp.int32))
        picked = results[expert_ids, slot_row].astype(jnp.float32)
        return jnp.sum(gates[step_index][:, :, None] * picked, axis=1).astype(jnp.bfloat16)

    return jnp.stack([one_step(step_index) for step_index in range(STEPS)])
```

```python
import functools

import jax
import jax.numpy as jnp
from jax import lax
from jax.experimental import pallas as pl
from jax.experimental.pallas import tpu as pltpu
from jax.sharding import PartitionSpec as P


def silu_glu(summed):
    return (jax.nn.silu(summed[:, 0]) * summed[:, 1]).astype(jnp.bfloat16)


def on_device(tokens, gate_up, w_down, routes, gates):
    steps_all, local_tokens, slab_width = tokens.shape
    top_count = routes.shape[2]
    groups = lax.axis_size("exp")
    experts = gate_up.shape[0] * groups
    capacity = max(2, 2 * local_tokens * top_count // experts)
    hidden_units = w_down.shape[1]
    row_count = groups * capacity
    weights_in = gate_up[0].reshape(slab_width, 2 * hidden_units)
    weights_out = w_down[0]
    labels = jnp.arange(experts * capacity, dtype=jnp.int32)
    expert_range = jnp.arange(experts, dtype=jnp.int32)
    expert_ids = routes[0].reshape(-1)
    onehot = (expert_ids[:, None] == expert_range[None, :]).astype(jnp.int32)
    before = jnp.cumsum(onehot, axis=0) - onehot
    slot_rank = jnp.sum(before * onehot, axis=1)
    target_row = expert_ids * capacity + slot_rank
    target_grid = target_row.reshape(local_tokens, top_count)
    placing = jnp.sum(
        (labels[:, None, None] == target_grid[None, :, :]).astype(jnp.int32), axis=2
    ).astype(jnp.bfloat16)
    outgoing = jnp.dot(placing, tokens[0], preferred_element_type=jnp.float32).astype(jnp.bfloat16)
    outgoing = outgoing.reshape(experts, capacity, slab_width)
    arrived = lax.all_to_all(outgoing, "exp", split_axis=0, concat_axis=0, tiled=True)
    partial_value = jnp.dot(
        arrived.reshape(row_count, slab_width), weights_in, preferred_element_type=jnp.float32
    )
    partial_value = partial_value.reshape(row_count, 2, hidden_units)
    shares = lax.psum_scatter(
        partial_value.astype(jnp.bfloat16), "rep", scatter_dimension=0, tiled=True
    ).astype(jnp.float32)
    hidden = silu_glu(shares)
    produced = jnp.dot(
        lax.all_gather(hidden, "rep", axis=0, tiled=True),
        weights_out,
        preferred_element_type=jnp.float32,
    )
    expert_out = produced.astype(jnp.bfloat16).reshape(groups, capacity, slab_width)
    returned = lax.all_to_all(expert_out, "exp", split_axis=0, concat_axis=0, tiled=True).reshape(
        experts * capacity, slab_width
    )
    picked = returned[target_row].reshape(local_tokens, top_count, slab_width).astype(jnp.float32)
    mixed_out = jnp.sum(gates[0][:, :, None] * picked, axis=1).astype(jnp.bfloat16)
    outputs = [mixed_out]
    return jnp.stack(outputs)


def fused_kernel(
    n, chunks, pieces, tok_ref, gu_ref, dn_ref, routes_ref, gates_ref, out_ref,
    xg, wgu, wdn, x2, pbuf, prec, hid, hfull, cbuf, crec, ybuf, yrec, zbuf, zrec,
    gu_sem, dn_sem, dz_s, dz_r, dy_s, dy_r, dc_s, dc_r,
    ps_s, ps_r, hs_s, hs_r, rc_s, rc_r, ry_s, ry_r, rz_s, rz_r,
):
    rep = lax.axis_index("rep")
    me = lax.axis_index("exp")
    zs = n // 4
    c, y, z = lax.rem(me, 2), lax.rem(me // 2, 2), me // 4
    rows, width = tok_ref.shape
    hidden_units = dn_ref.shape[0]
    cw, pw = hidden_units // chunks, width // pieces
    half = n * rows // 2
    other = 1 - rep
    core_peer = z * 4 + y * 2 + (1 - c)
    y_peer = z * 4 + (1 - y) * 2 + c

    def z_peer(d):
        return lax.rem(z + d, zs) * 4 + y * 2 + c

    def remote(src, dst, send, recv, to):
        return pltpu.make_async_remote_copy(
            src_ref=src, dst_ref=dst, send_sem=send, recv_sem=recv,
            device_id=to, device_id_type=pl.DeviceIdType.MESH,
        )

    barrier = pltpu.get_barrier_semaphore()
    peers = [(other, me), (rep, core_peer), (rep, y_peer)] + [(rep, z_peer(d)) for d in range(1, zs)]
    for peer in peers:
        pl.semaphore_signal(barrier, inc=1, device_id=peer, device_id_type=pl.DeviceIdType.MESH)

    def gu_copy(j):
        return pltpu.make_async_copy(
            gu_ref.at[:, :, pl.ds(pl.multiple_of(j * cw, 128), cw)], wgu.at[j], gu_sem.at[j]
        )

    def dn_copy(q):
        cols = pl.ds(q * pw, pw)
        return pltpu.make_async_copy(dn_ref.at[:, cols], wdn.at[:, cols], dn_sem.at[q])

    for j in range(chunks):
        gu_copy(j).start()
    for q in range(pieces):
        dn_copy(q).start()

    lane = lax.broadcasted_iota(jnp.int32, (rows, 128), 1)
    weight = jnp.zeros((rows, 128), jnp.float32)
    for k in range(routes_ref.shape[1]):
        hit = routes_ref[:, k : k + 1] == lax.rem(lane, n)
        weight = weight + jnp.where(hit, gates_ref[:, k : k + 1], 0.0)
    high = weight.astype(jnp.bfloat16).astype(jnp.float32)
    packed = jnp.where(lane < n, high, jnp.where(lane < 2 * n, weight - high, 0.0))
    xg[me, :, 0:width] = tok_ref[...]
    xg[me, :, width : width + 128] = packed.astype(jnp.bfloat16)
    pl.semaphore_wait(barrier, len(peers))

    def source(d, yy):
        return lax.rem(z - d + zs, zs) * 4 + yy * 2 + c

    def to_z(d):
        return remote(xg.at[me], xg.at[me], dz_s.at[d], dz_r.at[d], (rep, z_peer(d)))

    def to_y(d):
        slot = xg.at[source(d, y)]
        return remote(slot, slot, dy_s.at[d], dy_r.at[d], (rep, y_peer))

    def to_c(d, far):
        slot = xg.at[source(d, 1 - y if far else y)]
        at = d + zs * far
        return remote(slot, slot, dc_s.at[at], dc_r.at[at], (rep, core_peer))

    for d in range(1, zs):
        to_z(d).start()
    to_y(0).start()
    to_c(0, 0).start()
    for d in range(1, zs):
        to_z(d).wait_recv()
        to_y(d).start()
        to_c(d, 0).start()
    for d in range(zs):
        to_y(d).wait_recv()
        to_c(d, 1).start()
    for far in range(2):
        for d in range(zs):
            to_c(d, far).wait_recv()

    row_at = lax.broadcasted_iota(jnp.int32, (128, 512), 0)
    col_at = lax.broadcasted_iota(jnp.int32, (128, 512), 1)
    target = jnp.where(col_at < 256, 2 * row_at, 256 + 2 * row_at + 1)
    spread = jnp.where(col_at == target, 1.0, 0.0).astype(jnp.bfloat16)

    @pl.loop(0, width // 128)
    def _(b):
        part = xg[:, :, pl.ds(pl.multiple_of(b * 128, 128), 128)].reshape(2 * half, 128)
        both = jnp.dot(part, spread, preferred_element_type=jnp.float32).astype(jnp.bfloat16)
        cols = pl.ds(pl.multiple_of(b * 256, 256), 256)
        for h in range(2):
            x2[2 * h * half : (2 * h + 1) * half, cols] = both[h * half : (h + 1) * half, :256]
            x2[(2 * h + 1) * half : (2 * h + 2) * half, cols] = both[h * half : (h + 1) * half, 256:]

    def partial_send(j):
        return remote(pbuf.at[j, other], prec.at[j], ps_s.at[j], ps_r.at[j], (other, me))

    def hidden_send(j):
        return remote(hid.at[j, rep], hid.at[j, rep], hs_s.at[j], hs_r.at[j], (other, me))

    def hidden_recv(j):
        return remote(hid.at[j, other], hid.at[j, other], hs_s.at[j], hs_r.at[j], (other, me))

    def finish(j):
        partial_send(j).wait_recv()
        total = pbuf[j, rep].astype(jnp.float32) + prec[j].astype(jnp.float32)
        hid[j, rep] = (jax.nn.silu(total[:half]) * total[half:]).astype(jnp.bfloat16)
        hidden_send(j).start()

    lag = 2

    @pl.loop(0, chunks)
    def _(j):
        gu_copy(j).wait()
        weights = wgu[j].reshape(2 * width, cw)
        acc = jnp.dot(x2[...], weights, preferred_element_type=jnp.float32)
        pbuf[j] = acc.astype(jnp.bfloat16).reshape(2, 2 * half, cw)
        partial_send(j).start()

        @pl.when(j >= lag)
        def _():
            finish(j - lag)

    for j in range(chunks - lag, chunks):
        finish(j)
    for j in range(chunks):
        hidden_recv(j).wait_recv()
        hfull[:, j * cw : (j + 1) * cw] = hid[j].reshape(2 * half, cw)

    mark = lax.broadcasted_iota(jnp.int32, (2 * half, 128), 1)
    pair = xg[:, :, width : width + 128].reshape(2 * half, 128).astype(jnp.float32)
    scale = jnp.sum(jnp.where(lax.rem(mark, n) == me, pair, 0.0), axis=1, keepdims=True)

    def core_send(q):
        return remote(cbuf.at[q, 1 - c], crec.at[q], rc_s.at[q], rc_r.at[q], (rep, core_peer))

    def y_send(q):
        return remote(ybuf.at[q, 1 - y], yrec.at[q], ry_s.at[q], ry_r.at[q], (rep, y_peer))

    def z_send(q, d):
        return remote(
            zbuf.at[q, lax.rem(z + d, zs)], zrec.at[q, d], rz_s.at[q, d], rz_r.at[q, d], (rep, z_peer(d))
        )

    def produce(q):
        dn_copy(q).wait()
        made = jnp.dot(hfull[...], wdn[:, q * pw : (q + 1) * pw], preferred_element_type=jnp.float32)
        mixed = (made.astype(jnp.bfloat16).astype(jnp.float32) * scale).astype(jnp.bfloat16)
        mixed = mixed.reshape(n, rows, pw)
        for g in range(n):
            cbuf[q, g % 2, (g // 2) % 2, g // 4] = mixed[g]
        core_send(q).start()

    def over_core(q):
        core_send(q).wait_recv()
        ybuf[q] = (cbuf[q, c].astype(jnp.float32) + crec[q].astype(jnp.float32)).astype(jnp.bfloat16)
        y_send(q).start()

    def over_y(q):
        y_send(q).wait_recv()
        zbuf[q] = (ybuf[q, y].astype(jnp.float32) + yrec[q].astype(jnp.float32)).astype(jnp.bfloat16)
        for d in range(1, zs):
            z_send(q, d).start()

    def over_z(q):
        total = zbuf[q, z].astype(jnp.float32)
        for d in range(1, zs):
            z_send(q, d).wait_recv()
            total = total + zrec[q, d].astype(jnp.float32)
        out_ref[:, q * pw : (q + 1) * pw] = total.astype(jnp.bfloat16)

    for step in range(pieces + 3):
        for late, stage in enumerate((produce, over_core, over_y, over_z)):
            if 0 <= step - late < pieces:
                stage(step - late)

    for d in range(1, zs):
        to_z(d).wait_send()
    for d in range(zs):
        to_y(d).wait_send()
        for far in range(2):
            to_c(d, far).wait_send()
    for j in range(chunks):
        partial_send(j).wait_send()
        hidden_send(j).wait_send()
    for q in range(pieces):
        core_send(q).wait_send()
        y_send(q).wait_send()
        for d in range(1, zs):
            z_send(q, d).wait_send()


def fused_on_device(tokens, gate_up, w_down, routes, gates):
    n = lax.axis_size("exp")
    _, rows, width = tokens.shape
    hidden_units = w_down.shape[1]
    chunks, pieces = hidden_units // 256, 4
    pw, zs, half = width // pieces, n // 4, n * rows // 2
    bf16, dma = jnp.bfloat16, pltpu.SemaphoreType.DMA
    vmem = pl.BlockSpec(memory_space=pltpu.VMEM)
    anywhere = pl.BlockSpec(memory_space=pl.ANY)
    mixed_out = pl.pallas_call(
        functools.partial(fused_kernel, n, chunks, pieces),
        out_shape=jax.ShapeDtypeStruct((rows, width), bf16),
        in_specs=[vmem, anywhere, anywhere, vmem, vmem],
        out_specs=vmem,
        scratch_shapes=[
            pltpu.VMEM((n, rows, width + 128), bf16),
            pltpu.VMEM((chunks, width, 2, 256), bf16),
            pltpu.VMEM((hidden_units, width), bf16),
            pltpu.VMEM((4 * half, 2 * width), bf16),
            pltpu.VMEM((chunks, 2, 2 * half, 256), bf16),
            pltpu.VMEM((chunks, 2 * half, 256), bf16),
            pltpu.VMEM((chunks, 2, half, 256), bf16),
            pltpu.VMEM((2 * half, hidden_units), bf16),
            pltpu.VMEM((pieces, 2, 2, zs, rows, pw), bf16),
            pltpu.VMEM((pieces, 2, zs, rows, pw), bf16),
            pltpu.VMEM((pieces, 2, zs, rows, pw), bf16),
            pltpu.VMEM((pieces, zs, rows, pw), bf16),
            pltpu.VMEM((pieces, zs, rows, pw), bf16),
            pltpu.VMEM((pieces, zs, rows, pw), bf16),
            dma((chunks,)), dma((pieces,)),
            dma((zs,)), dma((zs,)), dma((zs,)), dma((zs,)), dma((2 * zs,)), dma((2 * zs,)),
            dma((chunks,)), dma((chunks,)), dma((chunks,)), dma((chunks,)),
            dma((pieces,)), dma((pieces,)), dma((pieces,)), dma((pieces,)),
            dma((pieces, zs)), dma((pieces, zs)),
        ],
        compiler_params=pltpu.CompilerParams(
            collective_id=0, has_side_effects=True, vmem_limit_bytes=67043328
        ),
    )(tokens[0], gate_up[0], w_down[0], routes[0], gates[0])
    return mixed_out[None]


def fits(mesh):
    return mesh.shape["rep"] == 2 and mesh.shape["exp"] % 4 == 0 and mesh.shape["exp"] <= 16


def solution(mesh):
    placed = (
        P(None, "exp", "rep"),
        P("exp", "rep", None, None),
        P("exp", None, "rep"),
        P(None, "exp", None),
        P(None, "exp", None),
    )
    return jax.shard_map(
        fused_on_device if fits(mesh) else on_device, mesh=mesh, in_specs=placed, out_specs=P(None, "exp", "rep"), check_vma=False
    )
```
